128 devices in a mesh: bx: 16 (over z, x), by: 8 (over y, core).
Axes of the slice: x: 4, y: 4, z: 4, core: 2. Of those that a mesh axis runs over, the one named last changes fastest.
Arguments:
- weights_re: float32 [1024, 16, 1024], P(None, 'bx', 'by'), may hold values from -3 to 3
- weights_im: float32 [1024, 16, 1024], P(None, 'bx', 'by'), may hold values from -3 to 3
Outputs:
- result_re: float32 [1024, 16, 1024], P(None, 'bx', 'by')
- result_im: float32 [1024, 16, 1024], P(None, 'bx', 'by')
The draws below stay inside these ranges and needn't reach their ends.
All inputs are finite; a program needn't handle non-finite values.
Results may differ from the reference program's by a relative error of at most 0.0028.
Values sent between devices are 32-bit elements; how exact they have to be, the bound alone decides.
No kernel may reach another device: no remote copies, remote signals or barrier semaphores. Data moves between devices by JAX's collectives and lax.ppermute only.
A program may use at most 64 MiB of HBM per device.

```python
import jax
import jax.numpy as jnp
from jax import lax

N_FREQ = 16384
CHEB = 8
FX = 32
FY = 32
FREQ_BOXES = 1024
SOURCE_BOXES = 16
N_BX = 16


def steps_of(own_key, shape, shards, low, high):
    factor_of = 1.0
    for dim, shards_of in shards:
        steps = jax.random.uniform(jax.random.fold_in(jax.random.fold_in(own_key, 6), dim), (shards_of,), jnp.float32, low / len(shards), high / len(shards))
        factor_of = factor_of * jnp.repeat(jnp.exp(steps), shape[dim] // shards_of).reshape((-1,) + (1,) * (len(shape) - 1 - dim))
    return factor_of


def centred(key, extent, scale, bound, shards=(), kind=jnp.bfloat16):
    level = steps_of(key, extent, shards, -0.22, 0.18) if shards else 1.0
    result = jax.random.normal(key, extent, jnp.float32) * scale * level
    return jnp.minimum(jnp.maximum(result, -bound), bound).astype(kind)


def setup_inputs(seed: int = 0) -> dict:
    arg_keys = jax.random.split(jax.random.key(seed), 3)
    weights_re = centred(arg_keys[0], (FREQ_BOXES, SOURCE_BOXES, SOURCE_BOXES * CHEB * CHEB), 0.5, 3.0, ((1, 16), (2, 8)), jnp.float32)
    weights_im = centred(arg_keys[1], (FREQ_BOXES, SOURCE_BOXES, SOURCE_BOXES * CHEB * CHEB), 0.5, 3.0, ((1, 16), (2, 8)), jnp.float32)
    return {"weights_re": weights_re, "weights_im": weights_im}


def cheb_nodes(cheb_count):
    index_vals = jnp.arange(cheb_count, dtype=jnp.float32)
    node_values = jnp.cos(jnp.pi * (2.0 * index_vals + 1.0) / (2.0 * cheb_count)) / 2.0
    node_high = jnp.floor(node_values * 1024.0) / 1024.0
    node_low = node_values - node_high
    return (node_values, node_high, node_low)

def lagrange_table(cheb_count):
    node_values = cheb_nodes(cheb_count)[0]
    side_offset = jnp.arange(2, dtype=jnp.float32) - 0.5
    child_points = side_offset[:, None] / 2.0 + node_values[None, :] / 2.0
    numerator = child_points[:, :, None, None] - node_values[None, None, None, :]
    diagonal_mask = jnp.eye(cheb_count, dtype=bool)
    denominator = jnp.where(diagonal_mask, 1.0, node_values[:, None] - node_values[None, :])
    factor_table = jnp.where(diagonal_mask[None, None], 1.0, numerator / denominator[None, None])
    lagrange_values = jnp.prod(factor_table, axis=3)
    product_table = jnp.einsum('asi,bzj->abszij', lagrange_values, lagrange_values, precision=lax.Precision.HIGHEST)
    return product_table.reshape(2, 2, cheb_count * cheb_count, cheb_count * cheb_count)

def fraction(values):
    return values - jnp.floor(values)

def phase_pair(center_x, center_y, width, freq_x, freq_y, cheb_count):
    node_values, node_high, node_low = cheb_nodes(cheb_count)
    along_x = jnp.repeat(node_values, cheb_count)
    along_y = jnp.tile(node_values, cheb_count)
    high_x = jnp.repeat(node_high, cheb_count)
    high_y = jnp.tile(node_high, cheb_count)
    low_x = jnp.repeat(node_low, cheb_count)
    low_y = jnp.tile(node_low, cheb_count)
    step_x = width * freq_x
    step_y = width * freq_y
    point_x = center_x + width * along_x
    point_y = center_y + width * along_y
    speed_x = (2.0 + jnp.sin(2.0 * jnp.pi * point_x) * jnp.sin(2.0 * jnp.pi * point_y)) / 16.0
    speed_y = (2.0 + jnp.cos(2.0 * jnp.pi * point_x) * jnp.cos(2.0 * jnp.pi * point_y)) / 16.0
    radial = jnp.sqrt((speed_x * freq_x) ** 2 + (speed_y * freq_y) ** 2)
    cycle_total = fraction(center_x * freq_x) + fraction(high_x * step_x) + low_x * step_x
    cycle_total = cycle_total + fraction(center_y * freq_y) + fraction(high_y * step_y) + low_y * step_y
    cycle_total = cycle_total + radial
    phase_angle = 2.0 * jnp.pi * fraction(cycle_total)
    return (jnp.cos(phase_angle), jnp.sin(phase_angle))

def butterfly_block(real_part, imag_part, freq_col, freq_row, box_count, cheb_count):
    point_count = cheb_count * cheb_count
    row_count = real_part.shape[0]
    level_count = box_count.bit_length() - 1
    interp = lagrange_table(cheb_count)
    current_re = real_part[:, None, None]
    current_im = imag_part[:, None, None]
    position_x = jnp.zeros((1,), jnp.float32)
    position_y = jnp.zeros((1,), jnp.float32)
    new_bits = jnp.arange(2, dtype=jnp.float32)
    for level_index in range(level_count):
        span_size = 2 ** level_index
        half_count = box_count // (2 * span_size)
        child_width = span_size / box_count
        parent_width = 2.0 * child_width
        width_x = N_FREQ / (FX * 2 * span_size)
        width_y = N_FREQ / (FY * 2 * span_size)
        index_x = freq_col[:, None, None] * (2 * span_size) + 2.0 * position_x[None, None, :] + new_bits[None, :, None]
        index_y = freq_row[:, None, None] * (2 * span_size) + 2.0 * position_y[None, None, :] + new_bits[None, :, None]
        wave_x = -N_FREQ / 2.0 + (index_x + 0.5) * width_x
        wave_y = -N_FREQ / 2.0 + (index_y + 0.5) * width_y
        parent_center = (jnp.arange(half_count, dtype=jnp.float32) + 0.5) * parent_width
        child_center = parent_center[:, None] + (new_bits[None, :] - 0.5) * child_width
        cos_in, sin_in = phase_pair(child_center[None, None, None, None, None, :, :, None, None, None], child_center[None, None, None, None, None, None, None, :, :, None], child_width, wave_x[:, :, :, None, None, None, None, None, None, None], wave_y[:, None, None, :, :, None, None, None, None, None], cheb_count)
        grid_re = current_re.reshape(row_count, span_size, span_size, half_count, 2, half_count, 2, point_count)[:, None, :, None]
        grid_im = current_im.reshape(row_count, span_size, span_size, half_count, 2, half_count, 2, point_count)[:, None, :, None]
        mixed_re = grid_re * cos_in - grid_im * sin_in
        mixed_im = grid_re * sin_in + grid_im * cos_in
        sum_re = jnp.einsum('bjaknpxqys,xyst->bjaknpqt', mixed_re, interp, precision=lax.Precision.HIGHEST)
        sum_im = jnp.einsum('bjaknpxqys,xyst->bjaknpqt', mixed_im, interp, precision=lax.Precision.HIGHEST)
        cos_out, sin_out = phase_pair(parent_center[None, None, None, None, None, :, None, None], parent_center[None, None, None, None, None, None, :, None], parent_width, wave_x[:, :, :, None, None, None, None, None], wave_y[:, None, None, :, :, None, None, None], cheb_count)
        new_re = sum_re * cos_out + sum_im * sin_out
        new_im = sum_im * cos_out - sum_re * sin_out
        current_re = new_re.reshape(row_count, 2 * span_size, 2 * span_size, half_count, half_count, point_count)
        current_im = new_im.reshape(row_count, 2 * span_size, 2 * span_size, half_count, half_count, point_count)
        position_x = jnp.concatenate([2.0 * position_x, 2.0 * position_x + 1.0])
        position_y = jnp.concatenate([2.0 * position_y, 2.0 * position_y + 1.0])
    return (current_re.reshape(row_count, box_count, box_count * point_count), current_im.reshape(row_count, box_count, box_count * point_count))

def reference(weights_re, weights_im):
    freq_total = FX * FY
    box_count = N_BX
    point_count = CHEB * CHEB
    block_rows = 64
    freq_index = jnp.arange(freq_total, dtype=jnp.int32)
    freq_col = (freq_index // FY).astype(jnp.float32)
    freq_row = (freq_index % FY).astype(jnp.float32)
    block_count = freq_total // block_rows
    real_blocks = weights_re.reshape(block_count, block_rows, box_count, box_count, point_count)
    imag_blocks = weights_im.reshape(block_count, block_rows, box_count, box_count, point_count)
    outputs = lax.map(lambda block_items: butterfly_block(block_items[0], block_items[1], block_items[2], block_items[3], box_count, CHEB), (real_blocks, imag_blocks, freq_col.reshape(block_count, block_rows), freq_row.reshape(block_count, block_rows)))
    result_re = outputs[0].reshape(freq_total, box_count, box_count * point_count)
    result_im = outputs[1].reshape(freq_total, box_count, box_count * point_count)
    return (result_re, result_im)
```

```python
import jax
import jax.numpy as jnp
import numpy as np
from jax import lax
from jax.experimental import pallas as pl
from jax.experimental.pallas import tpu as pltpu
from jax.sharding import PartitionSpec as P

N_FREQ = 16384
CHEB = 8
FX = 32
FY = 32
BOXES = 16
LEVELS = 4
POINTS = CHEB * CHEB
LANES = 2 * POINTS
ROWS = 8


def _fit(function, count):
    grid = np.cos(np.pi * (np.arange(count) + 0.5) / count) * 0.125 + 0.125
    return [float(c) for c in np.polyfit(grid, function(np.sqrt(grid)), count - 1)]


SIN_TERMS = _fit(lambda u: 2.0 * np.sin(np.pi * u) / u, 6)
COS_TERMS = _fit(lambda u: np.cos(np.pi * u), 6)


def horner(terms, value):
    total = terms[0] * value + terms[1]
    for term in terms[2:]:
        total = total * value + term
    return total


def turn(cycles):
    rest = cycles - jnp.round(cycles)
    square = rest * rest
    twice_sin = rest * horner(SIN_TERMS, square)
    half_cos = horner(COS_TERMS, square)
    return 1.0 - 0.5 * (twice_sin * twice_sin), twice_sin * half_cos


def nodes():
    value = (np.cos(np.pi * (2.0 * np.arange(CHEB) + 1.0) / (2.0 * CHEB)) / 2.0).astype(np.float32)
    high = (np.floor(value * np.float32(1024.0)) / np.float32(1024.0)).astype(np.float32)
    return value, high, value - high


def node_rows():
    value, high, low = nodes()
    lane = np.arange(LANES)
    first, second = lane // CHEB % CHEB, lane % CHEB
    rows = [value[first], value[second], high[first], low[first], high[second], low[second], lane // POINTS]
    rows.append(np.zeros(LANES))
    return np.stack(rows).astype(np.float32)


def lagrange_table():
    value = jnp.asarray(nodes()[0])
    side = jnp.arange(2, dtype=jnp.float32) - 0.5
    child = side[:, None] / 2.0 + value[None, :] / 2.0
    numerator = child[:, :, None, None] - value[None, None, None, :]
    diagonal = jnp.eye(CHEB, dtype=bool)
    denominator = jnp.where(diagonal, 1.0, value[:, None] - value[None, :])
    factor = jnp.where(diagonal[None, None], 1.0, numerator / denominator[None, None])
    return jnp.prod(factor, axis=3)


def interp_blocks():
    table = lagrange_table()
    interp = jnp.einsum("asi,bzj->abszij", table, table, precision=lax.Precision.HIGHEST)
    interp = interp.reshape(2, 2 * POINTS, POINTS)
    zero = jnp.zeros_like(interp)
    block = jnp.concatenate(
        [jnp.concatenate([interp, zero], axis=2), jnp.concatenate([zero, interp], axis=2)], axis=1
    )
    high = lax.reduce_precision(block, 8, 7)
    low = block - high
    return jnp.concatenate([high, low], axis=2).astype(jnp.bfloat16)


def path_offset(level, path):
    return sum((2 * (path >> bit & 1) - 1) * (N_FREQ // FX / 4) / 2**bit for bit in range(level))


def path_base(level):
    return 2**level - 1


def boxes_at(level):
    return BOXES >> level


def point_base(level):
    return sum((boxes_at(at) // 2) ** 2 for at in range(level))


def table_kernel(owner_ref, node_ref, t0c, t0s, t1c, t1s, t2c, t2s, t3c, t3s, fc, fs, sq1, sq2, sqp, pp, qq, lin):
    shape = (ROWS, LANES)
    row = lambda index: jnp.broadcast_to(node_ref[index : index + 1, :], shape)
    owner = owner_ref[0]
    fx = (owner // (FY // ROWS)).astype(jnp.float32)
    fy0 = (owner % (FY // ROWS) * ROWS).astype(jnp.float32)
    width = N_FREQ / FX
    sub = lax.broadcasted_iota(jnp.int32, shape, 0).astype(jnp.float32)
    k1 = jnp.full(shape, -N_FREQ / 2.0 + (fx + 0.5) * width, jnp.float32)
    k2 = -N_FREQ / 2.0 + (fy0 + sub + 0.5) * width
    for level in range(LEVELS + 1):
        for path in range(2**level):
            off = path_offset(level, path)
            sq1[path_base(level) + path] = (k1 + off) * (k1 + off)
            sq2[path_base(level) + path] = (k2 + off) * (k2 + off)
    upper = row(6) > 0.5
    for level in range(LEVELS + 1):
        n = boxes_at(level)
        w = 1.0 / n
        across, down = max(n // 2, 1), max(n // 2, 1)
        part_x = [turn((sx + 0.5) * w + w * row(0)) for sx in range(across)]
        part_y = []
        for pair in range(down):
            center = (2 * pair + row(6) + 0.5) * w if level < LEVELS else 0.5
            part_y.append(turn(center + w * row(1)))
        for sx in range(across):
            for pair in range(down):
                c1 = (2.0 + part_x[sx][1] * part_y[pair][1]) / 16.0
                c2 = (2.0 + part_x[sx][0] * part_y[pair][0]) / 16.0
                at = point_base(level) + sx * down + pair
                pp[at] = c1 * c1
                qq[at] = c2 * c2

    def frac(v):
        return v - jnp.floor(v)

    w = 1.0 / BOXES
    for jx in range(2):
        for jy in range(2):
            s1 = w * (k1 + path_offset(1, jx))
            s2 = w * (k2 + path_offset(1, jy))
            along = frac(row(2) * s1) + row(3) * s1 + frac(row(4) * s2) + row(5) * s2
            lin[2 * jx + jy] = along
            lin[4 + 2 * jx + jy] = (N_FREQ / FX / 4) / BOXES * ((2 * jx - 1) * row(0) + (2 * jy - 1) * row(1))

    @pl.loop(0, 8)
    def _(sx):
        for pair in range(8):
            p, q = pp[sx * 8 + pair], qq[sx * 8 + pair]
            for jx in range(2):
                for jy in range(2):
                    r = jnp.sqrt(p * sq1[1 + jx] + q * sq2[1 + jy])
                    c, s = turn(r - jnp.round(r) + lin[2 * jx + jy])
                    at = (2 * jx + jy) * 64 + sx * 8 + pair
                    t0c[at] = c
                    t0s[at] = s

    def level_of(level, ax, ay, sx, pair, out_c, out_s):
        n = boxes_at(level)
        half, span = n // 2, 2**level
        point = point_base(level) + sx * half + pair
        p, q = pp[point], qq[point]
        base = path_base(level)
        r0 = jnp.sqrt(p * sq1[base + ax] + q * sq2[base + ay])
        nxt = path_base(level + 1)
        for jx in range(2):
            for jy in range(2):
                j = 2 * jx + jy
                r = jnp.sqrt(p * sq1[nxt + ax + jx * span] + q * sq2[nxt + ay + jy * span])
                c, s = turn((r - r0) + lin[4 + j])
                path = j * span * span + ax * span + ay
                if level < 3:
                    at = (path * half + sx) * half + pair
                    out_c[at] = c
                    out_s[at] = s
                else:
                    out_c[2 * path] = c
                    out_s[2 * path] = s
                    out_c[2 * path + 1] = pltpu.roll(c, POINTS, 1)
                    out_s[2 * path + 1] = pltpu.roll(s, POINTS, 1)

    @pl.loop(0, 16)
    def _(step):
        a, sx = step // 4, step % 4
        for pair in range(4):
            level_of(1, a // 2, a % 2, sx, pair, t1c, t1s)

    @pl.loop(0, 16)
    def _(a):
        for sx in range(2):
            for pair in range(2):
                level_of(2, a // 4, a % 4, sx, pair, t2c, t2s)

    @pl.loop(0, 16)
    def _(step):
        for a in range(4):
            level_of(3, step // 2, step % 2 * 4 + a, 0, 0, t3c, t3s)

    base = path_base(LEVELS)
    for pair in range(8):
        off = jnp.where(upper, path_offset(LEVELS, 2 * pair + 1), path_offset(LEVELS, 2 * pair))
        k = k2 + off
        sqp[pair] = k * k
        lin[8 + pair] = frac(row(4) * k) + row(5) * k
    for path in range(16):
        k = k1 + path_offset(LEVELS, path)
        lin[16 + path] = frac(row(2) * k) + row(3) * k

    @pl.loop(0, 16)
    def _(ax):
        p, q = pp[point_base(LEVELS)], qq[point_base(LEVELS)]
        for pair in range(8):
            r = jnp.sqrt(p * sq1[base + ax] + q * sqp[pair])
            c, s = turn(r - jnp.round(r) + lin[16 + ax] + lin[8 + pair])
            fc[ax * 8 + pair] = c
            fs[ax * 8 + pair] = s


def merge_kernel(data_ref, w_ref, t0c, t0s, t1c, t1s, t2c, t2s, t3c, t3s, fc, fs, out_ref, ar, ai, br, bi, lhs):
    tables = ((t0c, t0s), (t1c, t1s), (t2c, t2s), (t3c, t3s))
    buffers = (None, (ar, ai), (br, bi), (ar, ai))

    for level in range(LEVELS):
        n = boxes_at(level)
        half, span = n // 2, 2**level
        cos_ref, sin_ref = tables[level]

        def load(index, level=level):
            if level == 0:
                return data_ref[index, 0:ROWS], data_ref[index, ROWS : 2 * ROWS]
            return buffers[level][0][index], buffers[level][1][index]

        def source(q, cx, e, level=level, n=n, half=half):
            if level == 3:
                index = (2 * q + e) * 2 + cx
                return index, index
            quarter = n // 4
            m, pair = q // quarter, 2 * (q % quarter) + e
            a, sx = m // half, 2 * (m % half) + cx
            index = (a * n + sx) * half + pair
            if sx >= half:
                sx, pair = sx - half, (pair + quarter) % half
            return index, (a * half + sx) * half + pair

        count = half * half * span * span if level < 3 else 2 * span * span

        @pl.loop(0, 4)
        def _(j, level=level, n=n, half=half, span=span, load=load, source=source, count=count,
              cos_ref=cos_ref, sin_ref=sin_ref):
            jx, jy = j // 2, j % 2
            for part in range(2):
                for cx in range(2):
                    for e in range(2):
                        for i in range(0, 16, 2):
                            pieces = []
                            for q in (16 * part + i, 16 * part + i + 1):
                                index, factor = source(q, cx, e)
                                xr, xi = load(index)
                                c, s = cos_ref[j * count + factor], sin_ref[j * count + factor]
                                pieces.append((xr * c - xi * s, xr * s + xi * c))
                            for which in range(2):
                                value = jnp.concatenate([pieces[0][which], pieces[1][which]], axis=0)
                                high = value.astype(jnp.bfloat16)
                                low = (value - high.astype(jnp.float32)).astype(jnp.bfloat16)
                                at = 128 * which + 8 * i
                                lhs[cx, pl.ds(at, 16), LANES * e : LANES * (e + 1)] = high
                                lhs[cx, pl.ds(256 + at, 16), LANES * e : LANES * (e + 1)] = low
                total = jnp.dot(lhs[0], w_ref[0], preferred_element_type=jnp.float32)
                total = total + jnp.dot(lhs[1], w_ref[1], preferred_element_type=jnp.float32)
                both = total[0:256, 0:LANES] + total[0:256, LANES:] + total[256:512, 0:LANES]
                for i in range(16):
                    q = 16 * part + i
                    re, im = both[8 * i : 8 * i + 8], both[128 + 8 * i : 128 + 8 * i + 8]
                    if level < 3:
                        block = n * n // 8
                        a, rest = q // block, q % block
                        ax, ay = a // span, a % span
                        at = ((jx * span + ax) * 2 * span + jy * span + ay) * block + rest
                        nr, ni = buffers[level + 1]
                        nr[at] = re
                        ni[at] = im
                    else:
                        ax, pair = q // 4, q % 4
                        at = (jx * 8 + ax) * 8 + jy * 4 + pair
                        c, s = fc[at], fs[at]
                        out_ref[at, 0:ROWS] = re * c + im * s
                        out_ref[at, ROWS : 2 * ROWS] = im * c - re * s


def tables(owner):
    f32 = jnp.float32
    vreg = (ROWS, LANES)
    sizes = (256, 256, 256, 512, 128)
    full = pl.BlockSpec(memory_space=pltpu.VMEM)
    return pl.pallas_call(
        table_kernel,
        out_shape=[jax.ShapeDtypeStruct((size,) + vreg, f32) for size in sizes for _ in range(2)],
        in_specs=[pl.BlockSpec(memory_space=pltpu.SMEM), full],
        out_specs=[full] * 10,
        scratch_shapes=[
            pltpu.VMEM((31,) + vreg, f32),
            pltpu.VMEM((31,) + vreg, f32),
            pltpu.VMEM((8,) + vreg, f32),
            pltpu.VMEM((88,) + vreg, f32),
            pltpu.VMEM((88,) + vreg, f32),
            pltpu.VMEM((32,) + vreg, f32),
        ],
        cost_estimate=pl.CostEstimate(flops=40_000_000, bytes_accessed=11 << 20, transcendentals=1_400_000),
        compiler_params=pltpu.CompilerParams(vmem_limit_bytes=20 << 20),
        name="phase_tables",
    )(owner, jnp.asarray(node_rows()))


def merge(data, weights, factors):
    f32 = jnp.float32
    vreg = (ROWS, LANES)
    full = pl.BlockSpec(memory_space=pltpu.VMEM)
    return pl.pallas_call(
        merge_kernel,
        out_shape=jax.ShapeDtypeStruct((128, 2 * ROWS, LANES), f32),
        in_specs=[full] * 12,
        out_specs=full,
        scratch_shapes=[pltpu.VMEM((128,) + vreg, f32)] * 4 + [pltpu.VMEM((2, 512, 256), jnp.bfloat16)],
        cost_estimate=pl.CostEstimate(flops=2_000_000_000, bytes_accessed=13 << 20, transcendentals=0),
        compiler_params=pltpu.CompilerParams(vmem_limit_bytes=32 << 20),
        name="merge_levels",
    )(data, weights, *factors)


def on_device(weights_re, weights_im):
    devices = 128
    owner = lax.axis_index("bx") * lax.axis_size("by") + lax.axis_index("by")
    sent = jnp.concatenate(
        [weights_re.reshape(devices, ROWS, LANES), weights_im.reshape(devices, ROWS, LANES)], axis=1
    )
    data = lax.all_to_all(sent, ("bx", "by"), 0, 0, tiled=True)
    factors = tables(owner.astype(jnp.int32).reshape(1))
    result = merge(data, interp_blocks(), factors)
    back = lax.all_to_all(result, ("bx", "by"), 0, 0, tiled=True)
    shape = (devices * ROWS, 1, LANES)
    return back[:, :ROWS].reshape(shape), back[:, ROWS:].reshape(shape)


def solution(mesh):
    specs = (P(None, "bx", "by"), P(None, "bx", "by"))
    return jax.shard_map(on_device, mesh=mesh, in_specs=specs, out_specs=specs, check_vma=False)
```

```python
import jax
import jax.numpy as jnp
import numpy as np
from jax import lax
from jax.experimental import pallas as pl
from jax.experimental.pallas import tpu as pltpu
from jax.sharding import PartitionSpec as P

N_FREQ = 16384
CHEB = 8
FX = 32
FY = 32
BOXES = 16
LEVELS = 4
POINTS = CHEB * CHEB
LANES = 2 * POINTS
ROWS = 8


def _fit(function, count):
    grid = np.cos(np.pi * (np.arange(count) + 0.5) / count) * 0.125 + 0.125
    return [float(c) for c in np.polyfit(grid, function(np.sqrt(grid)), count - 1)]


SIN_TERMS = _fit(lambda u: 2.0 * np.sin(np.pi * u) / u, 6)
COS_TERMS = _fit(lambda u: np.cos(np.pi * u), 6)


def horner(terms, value):
    total = terms[0] * value + terms[1]
    for term in terms[2:]:
        total = total * value + term
    return total


def turn(cycles):
    rest = cycles - jnp.round(cycles)
    square = rest * rest
    twice_sin = rest * horner(SIN_TERMS, square)
    half_cos = horner(COS_TERMS, square)
    return 1.0 - 0.5 * (twice_sin * twice_sin), twice_sin * half_cos


def nodes():
    value = (np.cos(np.pi * (2.0 * np.arange(CHEB) + 1.0) / (2.0 * CHEB)) / 2.0).astype(np.float32)
    high = (np.floor(value * np.float32(1024.0)) / np.float32(1024.0)).astype(np.float32)
    return value, high, value - high


def node_rows():
    value, high, low = nodes()
    lane = np.arange(LANES)
    first, second = lane // CHEB % CHEB, lane % CHEB
    rows = [value[first], value[second], high[first], low[first], high[second], low[second], lane // POINTS]
    rows.append(np.zeros(LANES))
    return np.stack(rows).astype(np.float32)


def path_offset(level, path):
    return sum((2 * (path >> bit & 1) - 1) * (N_FREQ // FX / 4) / 2**bit for bit in range(level))


def path_base(level):
    return 2**level - 1


def boxes_at(level):
    return BOXES >> level


def point_base(level):
    return sum((boxes_at(at) // 2) ** 2 for at in range(level))


TABLE_BASE = (0, 0, 256, 512, 1024)
TABLE_SIZE = 1152
TABLE_PARTS = ((0, 256), (256, 256), (512, 512), (1024, 128))


def interp_rows(node_ref, w_ref):
    shape = (LANES, LANES)
    source = lax.broadcasted_iota(jnp.int32, shape, 0)
    target = lax.broadcasted_iota(jnp.int32, shape, 1)
    value = nodes()[0]

    def pick(index):
        return sum(jnp.where(index == i, float(value[i]), 0.0) for i in range(CHEB))

    def lagrange(point, index):
        z = pick(index)
        total = None
        for j in range(CHEB):
            other = index != j
            factor = jnp.where(other, (point - float(value[j])) / jnp.where(other, z - float(value[j]), 1.0), 1.0)
            total = factor if total is None else total * factor
        return total

    first, second = source // CHEB % CHEB, source % CHEB
    row, column = target // CHEB % CHEB, target % CHEB
    cy = (source // POINTS).astype(jnp.float32)
    along_y = lagrange((cy - 0.5) / 2.0 + pick(second) / 2.0, column)
    for cx in range(2):
        block = lagrange((cx - 0.5) / 2.0 + pick(first) / 2.0, row) * along_y
        for pair in range(2):
            inside = target // POINTS == pair
            mine = jnp.where(inside, block, 0.0)
            high = mine.astype(jnp.bfloat16)
            low = (mine - high.astype(jnp.float32)).astype(jnp.bfloat16)
            at = (2 * cx + pair) * LANES
            w_ref[at : at + LANES, 0:LANES] = high
            w_ref[at : at + LANES, LANES : 2 * LANES] = low


def part_copies(make, part):
    at, size = TABLE_PARTS[part]
    return [make(which, pl.ds(at, size), 2 * part + which) for which in range(2)]


def table_kernel(owner_ref, node_ref, w_ref, cos0_ref, sin0_ref, rest_ref, sq1, sq2, sqp, pp, qq, lin, cos_ref, sin_ref, sems):
    def send(which, rows, sem):
        held = (cos_ref, sin_ref)[which]
        return pltpu.make_async_copy(held.at[rows], rest_ref.at[which, rows], sems.at[sem])

    def flush(part):
        for copy in part_copies(send, part):
            copy.start()

    shape = (ROWS, LANES)
    row = lambda index: jnp.broadcast_to(node_ref[index : index + 1, :], shape)
    owner = owner_ref[0]
    fx = (owner // (FY // ROWS)).astype(jnp.float32)
    fy0 = (owner % (FY // ROWS) * ROWS).astype(jnp.float32)
    width = N_FREQ / FX
    sub = lax.broadcasted_iota(jnp.int32, shape, 0).astype(jnp.float32)
    k1 = jnp.full(shape, -N_FREQ / 2.0 + (fx + 0.5) * width, jnp.float32)
    k2 = -N_FREQ / 2.0 + (fy0 + sub + 0.5) * width
    for level in range(LEVELS + 1):
        for path in range(2**level):
            off = path_offset(level, path)
            sq1[path_base(level) + path] = (k1 + off) * (k1 + off)
            sq2[path_base(level) + path] = (k2 + off) * (k2 + off)
    interp_rows(node_ref, w_ref)
    upper = row(6) > 0.5
    for level in range(LEVELS + 1):
        n = boxes_at(level)
        w = 1.0 / n
        across, down = max(n // 2, 1), max(n // 2, 1)
        part_x = [turn((sx + 0.5) * w + w * row(0)) for sx in range(across)]
        part_y = []
        for pair in range(down):
            center = (2 * pair + row(6) + 0.5) * w if level < LEVELS else 0.5
            part_y.append(turn(center + w * row(1)))
        for sx in range(across):
            for pair in range(down):
                c1 = (2.0 + part_x[sx][1] * part_y[pair][1]) / 16.0
                c2 = (2.0 + part_x[sx][0] * part_y[pair][0]) / 16.0
                at = point_base(level) + sx * down + pair
                pp[at] = c1 * c1
                qq[at] = c2 * c2

    def frac(v):
        return v - jnp.floor(v)

    w = 1.0 / BOXES
    for jx in range(2):
        for jy in range(2):
            s1 = w * (k1 + path_offset(1, jx))
            s2 = w * (k2 + path_offset(1, jy))
            along = frac(row(2) * s1) + row(3) * s1 + frac(row(4) * s2) + row(5) * s2
            lin[2 * jx + jy] = along
            lin[4 + 2 * jx + jy] = (N_FREQ / FX / 4) / BOXES * ((2 * jx - 1) * row(0) + (2 * jy - 1) * row(1))

    @pl.loop(0, 8)
    def _(sx):
        for pair in range(8):
            p, q = pp[sx * 8 + pair], qq[sx * 8 + pair]
            for jx in range(2):
                for jy in range(2):
                    r = jnp.sqrt(p * sq1[1 + jx] + q * sq2[1 + jy])
                    c, s = turn(r - jnp.round(r) + lin[2 * jx + jy])
                    at = (2 * jx + jy) * 64 + sx * 8 + pair
                    cos0_ref[at] = c
                    sin0_ref[at] = s

    def level_of(level, ax, ay, sx, pair):
        start = TABLE_BASE[level]
        n = boxes_at(level)
        half, span = n // 2, 2**level
        point = point_base(level) + sx * half + pair
        p, q = pp[point], qq[point]
        base = path_base(level)
        r0 = jnp.sqrt(p * sq1[base + ax] + q * sq2[base + ay])
        nxt = path_base(level + 1)
        for jx in range(2):
            for jy in range(2):
                j = 2 * jx + jy
                r = jnp.sqrt(p * sq1[nxt + ax + jx * span] + q * sq2[nxt + ay + jy * span])
                c, s = turn((r - r0) + lin[4 + j])
                path = j * span * span + ax * span + ay
                if level < 3:
                    at = start + (path * half + sx) * half + pair
                    cos_ref[at] = c
                    sin_ref[at] = s
                else:
                    at = start + 2 * path
                    cos_ref[at] = c
                    sin_ref[at] = s
                    cos_ref[at + 1] = pltpu.roll(c, POINTS, 1)
                    sin_ref[at + 1] = pltpu.roll(s, POINTS, 1)

    @pl.loop(0, 16)
    def _(step):
        a, sx = step // 4, step % 4
        for pair in range(4):
            level_of(1, a // 2, a % 2, sx, pair)

    flush(0)

    @pl.loop(0, 16)
    def _(a):
        for sx in range(2):
            for pair in range(2):
                level_of(2, a // 4, a % 4, sx, pair)

    flush(1)

    @pl.loop(0, 16)
    def _(step):
        for a in range(4):
            level_of(3, step // 2, step % 2 * 4 + a, 0, 0)

    flush(2)

    base = path_base(LEVELS)
    for pair in range(8):
        off = jnp.where(upper, path_offset(LEVELS, 2 * pair + 1), path_offset(LEVELS, 2 * pair))
        k = k2 + off
        sqp[pair] = k * k
        lin[8 + pair] = frac(row(4) * k) + row(5) * k
    for path in range(16):
        k = k1 + path_offset(LEVELS, path)
        lin[16 + path] = frac(row(2) * k) + row(3) * k

    @pl.loop(0, 16)
    def _(ax):
        p, q = pp[point_base(LEVELS)], qq[point_base(LEVELS)]
        for pair in range(8):
            r = jnp.sqrt(p * sq1[base + ax] + q * sqp[pair])
            c, s = turn(r - jnp.round(r) + lin[16 + ax] + lin[8 + pair])
            cos_ref[TABLE_BASE[LEVELS] + ax * 8 + pair] = c
            sin_ref[TABLE_BASE[LEVELS] + ax * 8 + pair] = s

    flush(3)
    for part in range(4):
        for copy in part_copies(send, part):
            copy.wait()


def merge_kernel(data_ref, w_ref, cos0_ref, sin0_ref, rest_ref, out_ref, ar, ai, br, bi, lhs_a, lhs_b, cos_rest, sin_rest, sems):
    def fetch(which, rows, sem):
        held = (cos_rest, sin_rest)[which]
        return pltpu.make_async_copy(rest_ref.at[which, rows], held.at[rows], sems.at[sem])

    for part in range(4):
        for copy in part_copies(fetch, part):
            copy.start()
    buffers = (None, (ar, ai), (br, bi), (ar, ai))
    w = w_ref[...]

    for level in range(LEVELS):
        n = boxes_at(level)
        half, span = n // 2, 2**level
        quarter = n // 4
        cos_ref, sin_ref = (cos_rest, sin_rest) if level else (cos0_ref, sin0_ref)
        if level:
            for part in (level - 1,) if level < 3 else (2, 3):
                for copy in part_copies(fetch, part):
                    copy.wait()
        count = (half * half if level < 3 else 2) * span * span

        def load(index, level=level):
            if level == 0:
                return data_ref[index, 0:ROWS], data_ref[index, ROWS : 2 * ROWS]
            return buffers[level][0][index], buffers[level][1][index]

        def source(q, cx, e, level=level, n=n, half=half, quarter=quarter):
            if level == 3:
                index = (2 * q + e) * 2 + cx
                return index, index
            m, pair = q // quarter, 2 * (q % quarter) + e
            a, sx = m // half, 2 * (m % half) + cx
            index = (a * n + sx) * half + pair
            if sx >= half:
                sx, pair = sx - half, (pair + quarter) % half
            return index, (a * half + sx) * half + pair

        def mix(j, part, lhs, load=load, source=source, base=TABLE_BASE[level], count=count,
                cos_ref=cos_ref, sin_ref=sin_ref):
            for i in range(0, 16, 2):
                for cx in range(2):
                    for e in range(2):
                        pieces = []
                        for q in (16 * part + i, 16 * part + i + 1):
                            index, factor = source(q, cx, e)
                            xr, xi = load(index)
                            at = base + j * count + factor
                            c, s = cos_ref[at], sin_ref[at]
                            pieces.append((xr * c - xi * s, xr * s + xi * c))
                        lanes = slice(LANES * (2 * cx + e), LANES * (2 * cx + e + 1))
                        for which in range(2):
                            value = jnp.concatenate([pieces[0][which], pieces[1][which]], axis=0)
                            high = value.astype(jnp.bfloat16)
                            low = (value - high.astype(jnp.float32)).astype(jnp.bfloat16)
                            at = 32 * i + 32 * which
                            lhs[at : at + 16, lanes] = high
                            lhs[at + 16 : at + 32, lanes] = low

        def store(j, part, lhs, level=level, n=n, span=span):
            jx, jy = j // 2, j % 2
            total = jnp.dot(lhs[...], w, preferred_element_type=jnp.float32)
            for i in range(16):
                q = 16 * part + i
                parts = []
                for which in range(2):
                    at = 32 * (i - i % 2) + 32 * which + 8 * (i % 2)
                    high, low = total[at : at + 8], total[at + 16 : at + 24]
                    parts.append(high[:, 0:LANES] + high[:, LANES:] + low[:, 0:LANES])
                re, im = parts
                if level < 3:
                    block = n * n // 8
                    a, rest = q // block, q % block
                    ax, ay = a // span, a % span
                    at = ((jx * span + ax) * 2 * span + jy * span + ay) * block + rest
                    buffers[level + 1][0][at] = re
                    buffers[level + 1][1][at] = im
                else:
                    ax, pair = q // 4, q % 4
                    at = (jx * 8 + ax) * 8 + jy * 4 + pair
                    c, s = cos_rest[TABLE_BASE[LEVELS] + at], sin_rest[TABLE_BASE[LEVELS] + at]
                    out_ref[at, 0:ROWS] = re * c + im * s
                    out_ref[at, ROWS : 2 * ROWS] = im * c - re * s

        @pl.loop(0, 4)
        def _(j, mix=mix, store=store):
            mix(j, 0, lhs_a)
            mix(j, 1, lhs_b)
            store(j, 0, lhs_a)
            store(j, 1, lhs_b)


def tables(owner):
    f32 = jnp.float32
    vreg = (ROWS, LANES)
    full = pl.BlockSpec(memory_space=pltpu.VMEM)
    return pl.pallas_call(
        table_kernel,
        out_shape=[jax.ShapeDtypeStruct((4 * LANES, 2 * LANES), jnp.bfloat16)]
        + [jax.ShapeDtypeStruct((256,) + vreg, f32)] * 2
        + [jax.ShapeDtypeStruct((2, TABLE_SIZE) + vreg, f32)],
        in_specs=[pl.BlockSpec(memory_space=pltpu.SMEM), full],
        out_specs=[full] * 3 + [pl.BlockSpec(memory_space=pltpu.MemorySpace.HBM)],
        scratch_shapes=[pltpu.VMEM((size,) + vreg, f32) for size in (31, 31, 8, 88, 88, 32, TABLE_SIZE, TABLE_SIZE)]
        + [pltpu.SemaphoreType.DMA((8,))],
        cost_estimate=pl.CostEstimate(flops=40_000_000, bytes_accessed=11 << 20, transcendentals=1_400_000),
        compiler_params=pltpu.CompilerParams(vmem_limit_bytes=50 << 20),
        name="phase_tables",
    )(owner, jnp.asarray(node_rows()))


def merge(data, weights, cosines, sines, rest):
    f32 = jnp.float32
    vreg = (ROWS, LANES)
    full = pl.BlockSpec(memory_space=pltpu.VMEM)
    return pl.pallas_call(
        merge_kernel,
        out_shape=jax.ShapeDtypeStruct((128, 2 * ROWS, LANES), f32),
        in_specs=[full] * 4 + [pl.BlockSpec(memory_space=pltpu.MemorySpace.HBM)],
        out_specs=full,
        scratch_shapes=[pltpu.VMEM((128,) + vreg, f32)] * 4 + [pltpu.VMEM((512, 512), jnp.bfloat16)] * 2
        + [pltpu.VMEM((TABLE_SIZE,) + vreg, f32)] * 2
        + [pltpu.SemaphoreType.DMA((8,))],
        cost_estimate=pl.CostEstimate(flops=2_000_000_000, bytes_accessed=13 << 20, transcendentals=0),
        compiler_params=pltpu.CompilerParams(vmem_limit_bytes=47 << 20),
        name="merge_levels",
    )(data, weights, cosines, sines, rest)


def on_device(weights_re, weights_im):
    devices = 128
    owner = lax.axis_index("bx") * lax.axis_size("by") + lax.axis_index("by")
    sent = jnp.concatenate(
        [weights_re.reshape(devices, ROWS, LANES), weights_im.reshape(devices, ROWS, LANES)], axis=1
    )
    data = lax.all_to_all(sent, ("bx", "by"), 0, 0, tiled=True)
    result = merge(data, *tables(owner.astype(jnp.int32).reshape(1)))
    back = lax.all_to_all(result, ("bx", "by"), 0, 0, tiled=True)
    shape = (devices * ROWS, 1, LANES)
    return back[:, :ROWS].reshape(shape), back[:, ROWS:].reshape(shape)


def solution(mesh):
    specs = (P(None, "bx", "by"), P(None, "bx", "by"))
    return jax.shard_map(on_device, mesh=mesh, in_specs=specs, out_specs=specs, check_vma=False)
```

```python
import jax
import jax.numpy as jnp
import numpy as np
from jax import lax
from jax.experimental import pallas as pl
from jax.experimental.pallas import tpu as pltpu
from jax.sharding import PartitionSpec as P

N_FREQ = 16384
CHEB = 8
FX = 32
FY = 32
BOXES = 16
LEVELS = 4
POINTS = CHEB * CHEB
LANES = 2 * POINTS
ROWS = 8


def _fit(function, count):
    grid = np.cos(np.pi * (np.arange(count) + 0.5) / count) * 0.125 + 0.125
    return [float(c) for c in np.polyfit(grid, function(np.sqrt(grid)), count - 1)]


SIN_TERMS = _fit(lambda u: 2.0 * np.sin(np.pi * u) / u, 6)
COS_TERMS = _fit(lambda u: np.cos(np.pi * u), 6)


def horner(terms, value):
    total = terms[0] * value + terms[1]
    for term in terms[2:]:
        total = total * value + term
    return total


def turn(cycles):
    rest = cycles - jnp.round(cycles)
    square = rest * rest
    twice_sin = rest * horner(SIN_TERMS, square)
    half_cos = horner(COS_TERMS, square)
    return 1.0 - 0.5 * (twice_sin * twice_sin), twice_sin * half_cos


def nodes():
    value = (np.cos(np.pi * (2.0 * np.arange(CHEB) + 1.0) / (2.0 * CHEB)) / 2.0).astype(np.float32)
    high = (np.floor(value * np.float32(1024.0)) / np.float32(1024.0)).astype(np.float32)
    return value, high, value - high


def node_rows():
    value, high, low = nodes()
    lane = np.arange(LANES)
    first, second = lane // CHEB % CHEB, lane % CHEB
    rows = [value[first], value[second], high[first], low[first], high[second], low[second], lane // POINTS]
    rows.append(np.zeros(LANES))
    return np.stack(rows).astype(np.float32)


def path_offset(level, path):
    return sum((2 * (path >> bit & 1) - 1) * (N_FREQ // FX / 4) / 2**bit for bit in range(level))


def path_base(level):
    return 2**level - 1


def boxes_at(level):
    return BOXES >> level


def point_base(level):
    return sum((boxes_at(at) // 2) ** 2 for at in range(level))


TABLE_BASE = (0, 0, 256, 512, 1024)
TABLE_SIZE = 1152
TABLE_PARTS = ((0, 256), (256, 256), (512, 512), (1024, 128))


def interp_rows(node_ref, w_ref):
    shape = (LANES, LANES)
    source = lax.broadcasted_iota(jnp.int32, shape, 0)
    target = lax.broadcasted_iota(jnp.int32, shape, 1)
    value = nodes()[0]

    def pick(index):
        return sum(jnp.where(index == i, float(value[i]), 0.0) for i in range(CHEB))

    def lagrange(point, index):
        z = pick(index)
        total = None
        for j in range(CHEB):
            other = index != j
            factor = jnp.where(other, (point - float(value[j])) / jnp.where(other, z - float(value[j]), 1.0), 1.0)
            total = factor if total is None else total * factor
        return total

    first, second = source // CHEB % CHEB, source % CHEB
    row, column = target // CHEB % CHEB, target % CHEB
    cy = (source // POINTS).astype(jnp.float32)
    along_y = lagrange((cy - 0.5) / 2.0 + pick(second) / 2.0, column)
    for cx in range(2):
        block = lagrange((cx - 0.5) / 2.0 + pick(first) / 2.0, row) * along_y
        for pair in range(2):
            inside = target // POINTS == pair
            mine = jnp.where(inside, block, 0.0)
            high = mine.astype(jnp.bfloat16)
            low = (mine - high.astype(jnp.float32)).astype(jnp.bfloat16)
            at = (2 * cx + pair) * LANES
            w_ref[at : at + LANES, 0:LANES] = high
            w_ref[at : at + LANES, LANES : 2 * LANES] = low


def part_copies(make, part):
    at, size = TABLE_PARTS[part]
    return [make(which, pl.ds(at, size), 2 * part + which) for which in range(2)]


def table_kernel(owner_ref, node_ref, w_ref, cos0_ref, sin0_ref, rest_ref, sq1, sq2, sqp, pp, qq, lin, cos_ref, sin_ref, sems):
    def send(which, rows, sem):
        held = (cos_ref, sin_ref)[which]
        return pltpu.make_async_copy(held.at[rows], rest_ref.at[which, rows], sems.at[sem])

    def flush(part):
        for copy in part_copies(send, part):
            copy.start()

    shape = (ROWS, LANES)
    row = lambda index: jnp.broadcast_to(node_ref[index : index + 1, :], shape)
    owner = owner_ref[0]
    fx = (owner // (FY // ROWS)).astype(jnp.float32)
    fy0 = (owner % (FY // ROWS) * ROWS).astype(jnp.float32)
    width = N_FREQ / FX
    sub = lax.broadcasted_iota(jnp.int32, shape, 0).astype(jnp.float32)
    k1 = jnp.full(shape, -N_FREQ / 2.0 + (fx + 0.5) * width, jnp.float32)
    k2 = -N_FREQ / 2.0 + (fy0 + sub + 0.5) * width
    for level in range(LEVELS + 1):
        for path in range(2**level):
            off = path_offset(level, path)
            sq1[path_base(level) + path] = (k1 + off) * (k1 + off)
            sq2[path_base(level) + path] = (k2 + off) * (k2 + off)
    interp_rows(node_ref, w_ref)
    upper = row(6) > 0.5
    for level in range(LEVELS + 1):
        n = boxes_at(level)
        w = 1.0 / n
        across, down = max(n // 2, 1), max(n // 2, 1)
        part_x = [turn((sx + 0.5) * w + w * row(0)) for sx in range(across)]
        part_y = []
        for pair in range(down):
            center = (2 * pair + row(6) + 0.5) * w if level < LEVELS else 0.5
            part_y.append(turn(center + w * row(1)))
        for sx in range(across):
            for pair in range(down):
                c1 = (2.0 + part_x[sx][1] * part_y[pair][1]) / 16.0
                c2 = (2.0 + part_x[sx][0] * part_y[pair][0]) / 16.0
                at = point_base(level) + sx * down + pair
                pp[at] = c1 * c1
                qq[at] = c2 * c2

    def frac(v):
        return v - jnp.floor(v)

    w = 1.0 / BOXES
    for jx in range(2):
        for jy in range(2):
            s1 = w * (k1 + path_offset(1, jx))
            s2 = w * (k2 + path_offset(1, jy))
            along = frac(row(2) * s1) + row(3) * s1 + frac(row(4) * s2) + row(5) * s2
            lin[2 * jx + jy] = along
            lin[4 + 2 * jx + jy] = (N_FREQ / FX / 4) / BOXES * ((2 * jx - 1) * row(0) + (2 * jy - 1) * row(1))

    @pl.loop(0, 8)
    def _(sx):
        for pair in range(8):
            p, q = pp[sx * 8 + pair], qq[sx * 8 + pair]
            for jx in range(2):
                for jy in range(2):
                    r = jnp.sqrt(p * sq1[1 + jx] + q * sq2[1 + jy])
                    c, s = turn(r - jnp.round(r) + lin[2 * jx + jy])
                    at = (2 * jx + jy) * 64 + sx * 8 + pair
                    cos0_ref[at] = c
                    sin0_ref[at] = s

    def level_of(level, ax, ay, sx, pair):
        start = TABLE_BASE[level]
        n = boxes_at(level)
        half, span = n // 2, 2**level
        point = point_base(level) + sx * half + pair
        p, q = pp[point], qq[point]
        base = path_base(level)
        r0 = jnp.sqrt(p * sq1[base + ax] + q * sq2[base + ay])
        nxt = path_base(level + 1)
        for jx in range(2):
            for jy in range(2):
                j = 2 * jx + jy
                r = jnp.sqrt(p * sq1[nxt + ax + jx * span] + q * sq2[nxt + ay + jy * span])
                c, s = turn((r - r0) + lin[4 + j])
                path = j * span * span + ax * span + ay
                if level < 3:
                    at = start + (path * half + sx) * half + pair
                    cos_ref[at] = c
                    sin_ref[at] = s
                else:
                    at = start + 2 * path
                    cos_ref[at] = c
                    sin_ref[at] = s
                    cos_ref[at + 1] = pltpu.roll(c, POINTS, 1)
                    sin_ref[at + 1] = pltpu.roll(s, POINTS, 1)

    @pl.loop(0, 16)
    def _(step):
        a, sx = step // 4, step % 4
        for pair in range(4):
            level_of(1, a // 2, a % 2, sx, pair)

    flush(0)

    @pl.loop(0, 16)
    def _(a):
        for sx in range(2):
            for pair in range(2):
                level_of(2, a // 4, a % 4, sx, pair)

    flush(1)

    @pl.loop(0, 16)
    def _(step):
        for a in range(4):
            level_of(3, step // 2, step % 2 * 4 + a, 0, 0)

    flush(2)

    base = path_base(LEVELS)
    for pair in range(8):
        off = jnp.where(upper, path_offset(LEVELS, 2 * pair + 1), path_offset(LEVELS, 2 * pair))
        k = k2 + off
        sqp[pair] = k * k
        lin[8 + pair] = frac(row(4) * k) + row(5) * k
    for path in range(16):
        k = k1 + path_offset(LEVELS, path)
        lin[16 + path] = frac(row(2) * k) + row(3) * k

    @pl.loop(0, 16)
    def _(ax):
        p, q = pp[point_base(LEVELS)], qq[point_base(LEVELS)]
        for pair in range(8):
            r = jnp.sqrt(p * sq1[base + ax] + q * sqp[pair])
            c, s = turn(r - jnp.round(r) + lin[16 + ax] + lin[8 + pair])
            cos_ref[TABLE_BASE[LEVELS] + ax * 8 + pair] = c
            sin_ref[TABLE_BASE[LEVELS] + ax * 8 + pair] = s

    flush(3)
    for part in range(4):
        for copy in part_copies(send, part):
            copy.wait()


def merge_kernel(data_ref, w_ref, cos0_ref, sin0_ref, rest_ref, out_ref, ar, ai, br, bi, lhs_a, lhs_b, lhs_c, lhs_d, cos_rest, sin_rest, sems):
    def fetch(which, rows, sem):
        held = (cos_rest, sin_rest)[which]
        return pltpu.make_async_copy(rest_ref.at[which, rows], held.at[rows], sems.at[sem])

    for part in range(4):
        for copy in part_copies(fetch, part):
            copy.start()
    buffers = (None, (ar, ai), (br, bi), (ar, ai))
    for level in range(LEVELS):
        n = boxes_at(level)
        half, span = n // 2, 2**level
        quarter = n // 4
        cos_ref, sin_ref = (cos_rest, sin_rest) if level else (cos0_ref, sin0_ref)
        if level:
            for part in (level - 1,) if level < 3 else (2, 3):
                for copy in part_copies(fetch, part):
                    copy.wait()
        count = (half * half if level < 3 else 2) * span * span

        def load(index, level=level):
            if level == 0:
                return data_ref[index, 0:ROWS], data_ref[index, ROWS : 2 * ROWS]
            return buffers[level][0][index], buffers[level][1][index]

        def source(q, cx, e, level=level, n=n, half=half, quarter=quarter):
            if level == 3:
                index = (2 * q + e) * 2 + cx
                return index, index
            m, pair = q // quarter, 2 * (q % quarter) + e
            a, sx = m // half, 2 * (m % half) + cx
            index = (a * n + sx) * half + pair
            if sx >= half:
                sx, pair = sx - half, (pair + quarter) % half
            return index, (a * half + sx) * half + pair

        def mix(j, part, lhs, load=load, source=source, base=TABLE_BASE[level], count=count,
                cos_ref=cos_ref, sin_ref=sin_ref):
            for i in range(0, 16, 2):
                for cx in range(2):
                    for e in range(2):
                        pieces = []
                        for q in (16 * part + i, 16 * part + i + 1):
                            index, factor = source(q, cx, e)
                            xr, xi = load(index)
                            at = base + j * count + factor
                            c, s = cos_ref[at], sin_ref[at]
                            pieces.append((xr * c - xi * s, xr * s + xi * c))
                        k = 2 * cx + e
                        for which in range(2):
                            value = jnp.concatenate([pieces[0][which], pieces[1][which]], axis=0)
                            high = value.astype(jnp.bfloat16)
                            low = (value - high.astype(jnp.float32)).astype(jnp.bfloat16)
                            at = 32 * i + 32 * which
                            lhs[k, at : at + 16] = high
                            lhs[k, at + 16 : at + 32] = low

        def store(j, part, lhs, level=level, n=n, span=span):
            jx, jy = j // 2, j % 2
            rows = jnp.concatenate([lhs[k] for k in range(4)], axis=1)
            total = jnp.dot(rows, w_ref[...], preferred_element_type=jnp.float32)
            for i in range(16):
                q = 16 * part + i
                parts = []
                for which in range(2):
                    at = 32 * (i - i % 2) + 32 * which + 8 * (i % 2)
                    high, low = total[at : at + 8], total[at + 16 : at + 24]
                    parts.append(high[:, 0:LANES] + high[:, LANES:] + low[:, 0:LANES])
                re, im = parts
                if level < 3:
                    block = n * n // 8
                    a, rest = q // block, q % block
                    ax, ay = a // span, a % span
                    at = ((jx * span + ax) * 2 * span + jy * span + ay) * block + rest
                    buffers[level + 1][0][at] = re
                    buffers[level + 1][1][at] = im
                else:
                    ax, pair = q // 4, q % 4
                    at = (jx * 8 + ax) * 8 + jy * 4 + pair
                    c, s = cos_rest[TABLE_BASE[LEVELS] + at], sin_rest[TABLE_BASE[LEVELS] + at]
                    out_ref[at, 0:ROWS] = re * c + im * s
                    out_ref[at, ROWS : 2 * ROWS] = im * c - re * s

        @pl.loop(0, 2)
        def _(jx, mix=mix, store=store):
            mix(2 * jx, 0, lhs_a)
            mix(2 * jx, 1, lhs_b)
            store(2 * jx, 0, lhs_a)
            mix(2 * jx + 1, 0, lhs_c)
            store(2 * jx, 1, lhs_b)
            mix(2 * jx + 1, 1, lhs_d)
            store(2 * jx + 1, 0, lhs_c)
            store(2 * jx + 1, 1, lhs_d)


def tables(owner):
    f32 = jnp.float32
    vreg = (ROWS, LANES)
    full = pl.BlockSpec(memory_space=pltpu.VMEM)
    return pl.pallas_call(
        table_kernel,
        out_shape=[jax.ShapeDtypeStruct((4 * LANES, 2 * LANES), jnp.bfloat16)]
        + [jax.ShapeDtypeStruct((256,) + vreg, f32)] * 2
        + [jax.ShapeDtypeStruct((2, TABLE_SIZE) + vreg, f32)],
        in_specs=[pl.BlockSpec(memory_space=pltpu.SMEM), full],
        out_specs=[full] * 3 + [pl.BlockSpec(memory_space=pltpu.MemorySpace.HBM)],
        scratch_shapes=[pltpu.VMEM((size,) + vreg, f32) for size in (31, 31, 8, 88, 88, 32, TABLE_SIZE, TABLE_SIZE)]
        + [pltpu.SemaphoreType.DMA((8,))],
        cost_estimate=pl.CostEstimate(flops=40_000_000, bytes_accessed=11 << 20, transcendentals=1_400_000),
        compiler_params=pltpu.CompilerParams(vmem_limit_bytes=50 << 20),
        name="phase_tables",
    )(owner, jnp.asarray(node_rows()))


def merge(data, weights, cosines, sines, rest):
    f32 = jnp.float32
    vreg = (ROWS, LANES)
    full = pl.BlockSpec(memory_space=pltpu.VMEM)
    return pl.pallas_call(
        merge_kernel,
        out_shape=jax.ShapeDtypeStruct((128, 2 * ROWS, LANES), f32),
        in_specs=[full] * 4 + [pl.BlockSpec(memory_space=pltpu.MemorySpace.HBM)],
        out_specs=full,
        scratch_shapes=[pltpu.VMEM((128,) + vreg, f32)] * 4 + [pltpu.VMEM((4, 512, LANES), jnp.bfloat16)] * 4
        + [pltpu.VMEM((TABLE_SIZE,) + vreg, f32)] * 2
        + [pltpu.SemaphoreType.DMA((8,))],
        cost_estimate=pl.CostEstimate(flops=2_000_000_000, bytes_accessed=13 << 20, transcendentals=0),
        compiler_params=pltpu.CompilerParams(vmem_limit_bytes=47 << 20),
        name="merge_levels",
    )(data, weights, cosines, sines, rest)


def on_device(weights_re, weights_im):
    devices = 128
    owner = lax.axis_index("bx") * lax.axis_size("by") + lax.axis_index("by")
    sent = jnp.concatenate(
        [weights_re.reshape(devices, ROWS, LANES), weights_im.reshape(devices, ROWS, LANES)], axis=1
    )
    data = lax.all_to_all(sent, ("bx", "by"), 0, 0, tiled=True)
    result = merge(data, *tables(owner.astype(jnp.int32).reshape(1)))
    back = lax.all_to_all(result, ("bx", "by"), 0, 0, tiled=True)
    shape = (devices * ROWS, 1, LANES)
    return back[:, :ROWS].reshape(shape), back[:, ROWS:].reshape(shape)


def solution(mesh):
    specs = (P(None, "bx", "by"), P(None, "bx", "by"))
    return jax.shard_map(on_device, mesh=mesh, in_specs=specs, out_specs=specs, check_vma=False)
```

```python
import jax
import jax.numpy as jnp
import numpy as np
from jax import lax
from jax.experimental import pallas as pl
from jax.experimental.pallas import tpu as pltpu
from jax.sharding import PartitionSpec as P

N_FREQ = 16384
CHEB = 8
FX = 32
FY = 32
BOXES = 16
LEVELS = 4
POINTS = CHEB * CHEB
LANES = 2 * POINTS
ROWS = 8


def _fit(function, count):
    grid = np.cos(np.pi * (np.arange(count) + 0.5) / count) * 0.125 + 0.125
    return [float(c) for c in np.polyfit(grid, function(np.sqrt(grid)), count - 1)]


SIN_TERMS = _fit(lambda u: 2.0 * np.sin(np.pi * u) / u, 6)
COS_TERMS = _fit(lambda u: np.cos(np.pi * u), 6)


def horner(terms, value):
    total = terms[0] * value + terms[1]
    for term in terms[2:]:
        total = total * value + term
    return total


def turn(cycles):
    rest = cycles - jnp.round(cycles)
    square = rest * rest
    twice_sin = rest * horner(SIN_TERMS, square)
    half_cos = horner(COS_TERMS, square)
    return 1.0 - 0.5 * (twice_sin * twice_sin), twice_sin * half_cos


def nodes():
    value = (np.cos(np.pi * (2.0 * np.arange(CHEB) + 1.0) / (2.0 * CHEB)) / 2.0).astype(np.float32)
    high = (np.floor(value * np.float32(1024.0)) / np.float32(1024.0)).astype(np.float32)
    return value, high, value - high


def node_rows():
    value, high, low = nodes()
    lane = np.arange(LANES)
    first, second = lane // CHEB % CHEB, lane % CHEB
    rows = [value[first], value[second], high[first], low[first], high[second], low[second], lane // POINTS]
    rows.append(np.zeros(LANES))
    return np.stack(rows).astype(np.float32)


def path_offset(level, path):
    return sum((2 * (path >> bit & 1) - 1) * (N_FREQ // FX / 4) / 2**bit for bit in range(level))


def path_base(level):
    return 2**level - 1


def boxes_at(level):
    return BOXES >> level


def point_base(level):
    return sum((boxes_at(at) // 2) ** 2 for at in range(level))


TABLE_BASE = (0, 0, 256, 512, 1024)
TABLE_SIZE = 1152
STACK_PARTS = 2
TABLE_PARTS = ((0, 256), (256, 256), (512, 512), (1024, 128))


def interp_rows(node_ref, w_ref):
    shape = (LANES, LANES)
    source = lax.broadcasted_iota(jnp.int32, shape, 0)
    target = lax.broadcasted_iota(jnp.int32, shape, 1)
    value = nodes()[0]

    def pick(index):
        return sum(jnp.where(index == i, float(value[i]), 0.0) for i in range(CHEB))

    def lagrange(point, index):
        z = pick(index)
        total = None
        for j in range(CHEB):
            other = index != j
            factor = jnp.where(other, (point - float(value[j])) / jnp.where(other, z - float(value[j]), 1.0), 1.0)
            total = factor if total is None else total * factor
        return total

    first, second = source // CHEB % CHEB, source % CHEB
    row, column = target // CHEB % CHEB, target % CHEB
    cy = (source // POINTS).astype(jnp.float32)
    along_y = lagrange((cy - 0.5) / 2.0 + pick(second) / 2.0, column)
    for cx in range(2):
        block = lagrange((cx - 0.5) / 2.0 + pick(first) / 2.0, row) * along_y
        for pair in range(2):
            inside = target // POINTS == pair
            mine = jnp.where(inside, block, 0.0)
            high = mine.astype(jnp.bfloat16)
            low = (mine - high.astype(jnp.float32)).astype(jnp.bfloat16)
            at = (2 * cx + pair) * LANES
            w_ref[at : at + LANES, 0:LANES] = high
            w_ref[at : at + LANES, LANES : 2 * LANES] = low


def part_copies(make, part):
    at, size = TABLE_PARTS[part]
    return [make(which, pl.ds(at, size), 2 * part + which) for which in range(2)]


def table_kernel(owner_ref, node_ref, w_ref, cos0_ref, sin0_ref, rest_ref, sq1, sq2, sqp, pp, qq, lin, cos_ref, sin_ref, sems):
    def send(which, rows, sem):
        held = (cos_ref, sin_ref)[which]
        return pltpu.make_async_copy(held.at[rows], rest_ref.at[which, rows], sems.at[sem])

    def flush(part):
        for copy in part_copies(send, part):
            copy.start()

    shape = (ROWS, LANES)
    row = lambda index: jnp.broadcast_to(node_ref[index : index + 1, :], shape)
    owner = owner_ref[0]
    fx = (owner // (FY // ROWS)).astype(jnp.float32)
    fy0 = (owner % (FY // ROWS) * ROWS).astype(jnp.float32)
    width = N_FREQ / FX
    sub = lax.broadcasted_iota(jnp.int32, shape, 0).astype(jnp.float32)
    k1 = jnp.full(shape, -N_FREQ / 2.0 + (fx + 0.5) * width, jnp.float32)
    k2 = -N_FREQ / 2.0 + (fy0 + sub + 0.5) * width
    for level in range(LEVELS + 1):
        for path in range(2**level):
            off = path_offset(level, path)
            sq1[path_base(level) + path] = (k1 + off) * (k1 + off)
            sq2[path_base(level) + path] = (k2 + off) * (k2 + off)
    interp_rows(node_ref, w_ref)
    upper = row(6) > 0.5
    for level in range(LEVELS + 1):
        n = boxes_at(level)
        w = 1.0 / n
        across, down = max(n // 2, 1), max(n // 2, 1)
        part_x = [turn((sx + 0.5) * w + w * row(0)) for sx in range(across)]
        part_y = []
        for pair in range(down):
            center = (2 * pair + row(6) + 0.5) * w if level < LEVELS else 0.5
            part_y.append(turn(center + w * row(1)))
        for sx in range(across):
            for pair in range(down):
                c1 = (2.0 + part_x[sx][1] * part_y[pair][1]) / 16.0
                c2 = (2.0 + part_x[sx][0] * part_y[pair][0]) / 16.0
                at = point_base(level) + sx * down + pair
                pp[at] = c1 * c1
                qq[at] = c2 * c2

    def frac(v):
        return v - jnp.floor(v)

    w = 1.0 / BOXES
    for jx in range(2):
        for jy in range(2):
            s1 = w * (k1 + path_offset(1, jx))
            s2 = w * (k2 + path_offset(1, jy))
            along = frac(row(2) * s1) + row(3) * s1 + frac(row(4) * s2) + row(5) * s2
            lin[2 * jx + jy] = along
            lin[4 + 2 * jx + jy] = (N_FREQ / FX / 4) / BOXES * ((2 * jx - 1) * row(0) + (2 * jy - 1) * row(1))

    @pl.loop(0, 8)
    def _(sx):
        for pair in range(8):
            p, q = pp[sx * 8 + pair], qq[sx * 8 + pair]
            for jx in range(2):
                for jy in range(2):
                    r = jnp.sqrt(p * sq1[1 + jx] + q * sq2[1 + jy])
                    c, s = turn(r - jnp.round(r) + lin[2 * jx + jy])
                    at = (2 * jx + jy) * 64 + sx * 8 + pair
                    cos0_ref[at] = c
                    sin0_ref[at] = s

    def level_of(level, ax, ay, sx, pair):
        start = TABLE_BASE[level]
        n = boxes_at(level)
        half, span = n // 2, 2**level
        point = point_base(level) + sx * half + pair
        p, q = pp[point], qq[point]
        base = path_base(level)
        r0 = jnp.sqrt(p * sq1[base + ax] + q * sq2[base + ay])
        nxt = path_base(level + 1)
        for jx in range(2):
            for jy in range(2):
                j = 2 * jx + jy
                r = jnp.sqrt(p * sq1[nxt + ax + jx * span] + q * sq2[nxt + ay + jy * span])
                c, s = turn((r - r0) + lin[4 + j])
                path = j * span * span + ax * span + ay
                if level < 3:
                    at = start + (path * half + sx) * half + pair
                    cos_ref[at] = c
                    sin_ref[at] = s
                else:
                    at = start + 2 * path
                    cos_ref[at] = c
                    sin_ref[at] = s
                    cos_ref[at + 1] = pltpu.roll(c, POINTS, 1)
                    sin_ref[at + 1] = pltpu.roll(s, POINTS, 1)

    @pl.loop(0, 16)
    def _(step):
        a, sx = step // 4, step % 4
        for pair in range(4):
            level_of(1, a // 2, a % 2, sx, pair)

    flush(0)

    @pl.loop(0, 16)
    def _(a):
        for sx in range(2):
            for pair in range(2):
                level_of(2, a // 4, a % 4, sx, pair)

    flush(1)

    @pl.loop(0, 16)
    def _(step):
        for a in range(4):
            level_of(3, step // 2, step % 2 * 4 + a, 0, 0)

    flush(2)

    base = path_base(LEVELS)
    for pair in range(8):
        off = jnp.where(upper, path_offset(LEVELS, 2 * pair + 1), path_offset(LEVELS, 2 * pair))
        k = k2 + off
        sqp[pair] = k * k
        lin[8 + pair] = frac(row(4) * k) + row(5) * k
    for path in range(16):
        k = k1 + path_offset(LEVELS, path)
        lin[16 + path] = frac(row(2) * k) + row(3) * k

    @pl.loop(0, 16)
    def _(ax):
        p, q = pp[point_base(LEVELS)], qq[point_base(LEVELS)]
        for pair in range(8):
            r = jnp.sqrt(p * sq1[base + ax] + q * sqp[pair])
            c, s = turn(r - jnp.round(r) + lin[16 + ax] + lin[8 + pair])
            cos_ref[TABLE_BASE[LEVELS] + ax * 8 + pair] = c
            sin_ref[TABLE_BASE[LEVELS] + ax * 8 + pair] = s

    flush(3)
    for part in range(4):
        for copy in part_copies(send, part):
            copy.wait()


def merge_kernel(data_ref, w_ref, cos0_ref, sin0_ref, rest_ref, out_ref, ar, ai, br, bi, lhs_a, lhs_b, lhs_c, lhs_d, cos_rest, sin_rest, sems):
    def fetch(which, rows, sem):
        held = (cos_rest, sin_rest)[which]
        return pltpu.make_async_copy(rest_ref.at[which, rows], held.at[rows], sems.at[sem])

    for part in range(4):
        for copy in part_copies(fetch, part):
            copy.start()
    buffers = (None, (ar, ai), (br, bi), (ar, ai))
    for level in range(LEVELS):
        n = boxes_at(level)
        half, span = n // 2, 2**level
        quarter = n // 4
        cos_ref, sin_ref = (cos_rest, sin_rest) if level else (cos0_ref, sin0_ref)
        if level:
            for part in (level - 1,) if level < 3 else (2, 3):
                for copy in part_copies(fetch, part):
                    copy.wait()
        count = (half * half if level < 3 else 2) * span * span

        def load(index, level=level):
            if level == 0:
                return data_ref[index, 0:ROWS], data_ref[index, ROWS : 2 * ROWS]
            return buffers[level][0][index], buffers[level][1][index]

        def source(q, cx, e, level=level, n=n, half=half, quarter=quarter):
            if level == 3:
                index = (2 * q + e) * 2 + cx
                return index, index
            m, pair = q // quarter, 2 * (q % quarter) + e
            a, sx = m // half, 2 * (m % half) + cx
            index = (a * n + sx) * half + pair
            if sx >= half:
                sx, pair = sx - half, (pair + quarter) % half
            return index, (a * half + sx) * half + pair

        def mix(j, part, lhs, load=load, source=source, base=TABLE_BASE[level], count=count,
                cos_ref=cos_ref, sin_ref=sin_ref):
            for i in range(0, 16, 2):
                for cx in range(2):
                    for e in range(2):
                        pieces = []
                        for q in (16 * part + i, 16 * part + i + 1):
                            index, factor = source(q, cx, e)
                            xr, xi = load(index)
                            at = base + j * count + factor
                            c, s = cos_ref[at], sin_ref[at]
                            pieces.append((xr * c - xi * s, xr * s + xi * c))
                        k = 2 * cx + e
                        for which in range(2):
                            value = jnp.concatenate([pieces[0][which], pieces[1][which]], axis=0)
                            high = value.astype(jnp.bfloat16)
                            low = (value - high.astype(jnp.float32)).astype(jnp.bfloat16)
                            at = 32 * i + 32 * which
                            lhs[k, at : at + 16] = high
                            lhs[k, at + 16 : at + 32] = low

        def store(j, part, lhs, level=level, n=n, span=span):
            jx, jy = j // 2, j % 2
            rows = jnp.concatenate([lhs[k] for k in range(4)], axis=1)
            total = jnp.dot(rows, w_ref[...], preferred_element_type=jnp.float32)
            for i in range(16):
                q = 16 * part + i
                parts = []
                for which in range(2):
                    at = 32 * (i - i % 2) + 32 * which + 8 * (i % 2)
                    high, low = total[at : at + 8], total[at + 16 : at + 24]
                    parts.append(high[:, 0:LANES] + high[:, LANES:] + low[:, 0:LANES])
                re, im = parts
                if level < 3:
                    block = n * n // 8
                    a, rest = q // block, q % block
                    ax, ay = a // span, a % span
                    at = ((jx * span + ax) * 2 * span + jy * span + ay) * block + rest
                    buffers[level + 1][0][at] = re
                    buffers[level + 1][1][at] = im
                else:
                    ax, pair = q // 4, q % 4
                    at = (jx * 8 + ax) * 8 + jy * 4 + pair
                    c, s = cos_rest[TABLE_BASE[LEVELS] + at], sin_rest[TABLE_BASE[LEVELS] + at]
                    out_ref[at, 0:ROWS] = re * c + im * s
                    out_ref[at, ROWS : 2 * ROWS] = im * c - re * s

        @pl.loop(0, 2)
        def _(jx, mix=mix, store=store):
            mix(2 * jx, 0, lhs_a)
            mix(2 * jx, 1, lhs_b)
            store(2 * jx, 0, lhs_a)
            mix(2 * jx + 1, 0, lhs_c)
            store(2 * jx, 1, lhs_b)
            mix(2 * jx + 1, 1, lhs_d)
            store(2 * jx + 1, 0, lhs_c)
            store(2 * jx + 1, 1, lhs_d)


def tables(owner):
    f32 = jnp.float32
    vreg = (ROWS, LANES)
    full = pl.BlockSpec(memory_space=pltpu.VMEM)
    return pl.pallas_call(
        table_kernel,
        out_shape=[jax.ShapeDtypeStruct((4 * LANES, 2 * LANES), jnp.bfloat16)]
        + [jax.ShapeDtypeStruct((256,) + vreg, f32)] * 2
        + [jax.ShapeDtypeStruct((2, TABLE_SIZE) + vreg, f32)],
        in_specs=[pl.BlockSpec(memory_space=pltpu.SMEM), full],
        out_specs=[full] * 3 + [pl.BlockSpec(memory_space=pltpu.MemorySpace.HBM)],
        scratch_shapes=[pltpu.VMEM((size,) + vreg, f32) for size in (31, 31, 8, 88, 88, 32, TABLE_SIZE, TABLE_SIZE)]
        + [pltpu.SemaphoreType.DMA((8,))],
        cost_estimate=pl.CostEstimate(flops=40_000_000, bytes_accessed=11 << 20, transcendentals=1_400_000),
        compiler_params=pltpu.CompilerParams(vmem_limit_bytes=50 << 20),
        name="phase_tables",
    )(owner, jnp.asarray(node_rows()))


def merge(data, weights, cosines, sines, rest):
    f32 = jnp.float32
    vreg = (ROWS, LANES)
    full = pl.BlockSpec(memory_space=pltpu.VMEM)
    return pl.pallas_call(
        merge_kernel,
        out_shape=jax.ShapeDtypeStruct((128, 2 * ROWS, LANES), f32),
        in_specs=[full] * 4 + [pl.BlockSpec(memory_space=pltpu.MemorySpace.HBM)],
        out_specs=full,
        scratch_shapes=[pltpu.VMEM((128,) + vreg, f32)] * 4 + [pltpu.VMEM((4, 512, LANES), jnp.bfloat16)] * 4
        + [pltpu.VMEM((TABLE_SIZE,) + vreg, f32)] * 2
        + [pltpu.SemaphoreType.DMA((8,))],
        cost_estimate=pl.CostEstimate(flops=2_000_000_000, bytes_accessed=13 << 20, transcendentals=0),
        compiler_params=pltpu.CompilerParams(vmem_limit_bytes=47 << 20),
        name="merge_levels",
    )(data, weights, cosines, sines, rest)


def stack_kernel(re_ref, im_ref, out_ref, held, in_sems, out_sems):
    size = 128 // STACK_PARTS

    def inward(part, which):
        rows = pl.ds(part * size, size)
        source = (re_ref, im_ref)[which]
        return pltpu.make_async_copy(
            source.at[rows], held.at[rows, pl.ds(which * ROWS, ROWS)], in_sems.at[2 * part + which]
        )

    def outward(part):
        rows = pl.ds(part * size, size)
        return pltpu.make_async_copy(held.at[rows], out_ref.at[rows], out_sems.at[part])

    for part in range(STACK_PARTS):
        for which in range(2):
            inward(part, which).start()
    for part in range(STACK_PARTS):
        for which in range(2):
            inward(part, which).wait()
        outward(part).start()
    for part in range(STACK_PARTS):
        outward(part).wait()


def stacked(first, second):
    anywhere = pl.BlockSpec(memory_space=pl.ANY)
    return pl.pallas_call(
        stack_kernel,
        out_shape=jax.ShapeDtypeStruct((128, 2 * ROWS, LANES), jnp.float32),
        in_specs=[anywhere] * 2,
        out_specs=anywhere,
        scratch_shapes=[
            pltpu.VMEM((128, 2 * ROWS, LANES), jnp.float32),
            pltpu.SemaphoreType.DMA((2 * STACK_PARTS,)),
            pltpu.SemaphoreType.DMA((STACK_PARTS,)),
        ],
        cost_estimate=pl.CostEstimate(flops=0, bytes_accessed=2 << 20, transcendentals=0),
        compiler_params=pltpu.CompilerParams(vmem_limit_bytes=58 << 20),
        name="stack_parts",
    )(first, second)


def on_device(weights_re, weights_im):
    devices = 128
    owner = lax.axis_index("bx") * lax.axis_size("by") + lax.axis_index("by")
    sent = stacked(
        weights_re.reshape(devices, ROWS, LANES), weights_im.reshape(devices, ROWS, LANES)
    )
    data = lax.all_to_all(sent, ("bx", "by"), 0, 0, tiled=True)
    result = merge(data, *tables(owner.astype(jnp.int32).reshape(1)))
    back = lax.all_to_all(result, ("bx", "by"), 0, 0, tiled=True)
    shape = (devices * ROWS, 1, LANES)
    return back[:, :ROWS].reshape(shape), back[:, ROWS:].reshape(shape)


def solution(mesh):
    specs = (P(None, "bx", "by"), P(None, "bx", "by"))
    return jax.shard_map(on_device, mesh=mesh, in_specs=specs, out_specs=specs, check_vma=False)
```
